32 devices in a mesh: aux: 2 (over y), pair: 16 (over z, x, core).
Axes of the slice: x: 2, y: 2, z: 4, core: 2. Of those that a mesh axis runs over, the one named last changes fastest.
Arguments:
- density: bfloat16 [28800, 28800], P('aux', 'pair'), may hold values from -0.03125 to 0.03125
- cholesky: bfloat16 [512, 28800], P('pair', 'aux'), may hold values from -6 to 6
- virtual_orbitals: bfloat16 [3000, 1800], P('aux'), may hold values from -0.125 to 0.125
- occupied_orbitals: bfloat16 [128, 16], replicated, may hold values from -1.5 to 1.5
Outputs:
- back_transformed: bfloat16 [512, 128, 3000], P('pair', None, 'aux')
- lagrangian: float32 [16, 16], P(None, 'aux')
The draws below stay inside these ranges and needn't reach their ends.
All inputs are finite; a program needn't handle non-finite values.
Results may differ from the reference program's by a relative error of at most 0.0057.
Values may be sent and summed in bfloat16 or wider, within the bound.
No kernel may reach another device: no remote copies, remote signals or barrier semaphores. Data moves between devices by JAX's collectives and lax.ppermute only.
A program may use at most 128 MiB of HBM per device.

```python
import jax
import jax.numpy as jnp

NVIR = 1800
NAO = 3000
NCHOL = 512
NOCC = 16
AO_ROWS = 128
PAIRS = 28800


def block_levels(stream_key, shape, split, low, top_value):
    def one(position, blocks):
        steps = jax.random.uniform(jax.random.fold_in(jax.random.fold_in(stream_key, 6), position), (blocks,), jnp.float32, low / len(split), top_value / len(split))
        return jnp.repeat(jnp.exp(steps), shape[position] // blocks).reshape((-1,) + (1,) * (len(shape) - position - 1))

    factor_of = one(*split[0])
    for cut in split[1:]:
        factor_of = factor_of * one(*cut)
    return factor_of


def centred(own_key, extent, scale, limit, split=(), held_as=jnp.bfloat16):
    level = block_levels(own_key, extent, split, -0.22, 0.18) if split else 1.0
    array = jax.random.normal(own_key, extent, jnp.float32) * scale * level
    return jnp.minimum(jnp.maximum(array, -limit), limit).astype(held_as)


def setup_inputs(seed: int = 0) -> dict:
    key_list = jax.random.split(jax.random.key(seed), 5)
    density = centred(key_list[0], (PAIRS, PAIRS), PAIRS ** -0.5, 0.03125, ((0, 2), (1, 16)))
    cholesky = centred(key_list[1], (NCHOL, PAIRS), 1.0, 6.0, ((0, 16), (1, 2)))
    virtual_orbitals = centred(key_list[2], (NAO, NVIR), NVIR ** -0.5, 0.125, ((0, 2),))
    occupied_orbitals = centred(key_list[3], (AO_ROWS, NOCC), NOCC ** -0.5, 1.5)
    return dict(density=density, cholesky=cholesky, virtual_orbitals=virtual_orbitals, occupied_orbitals=occupied_orbitals)


def reference(density, cholesky, virtual_orbitals, occupied_orbitals):
    gamma = jnp.dot(cholesky, density, preferred_element_type=jnp.float32).astype(jnp.bfloat16)
    flat = gamma.reshape(NCHOL * NOCC, NVIR)
    half_done = jnp.dot(flat, virtual_orbitals.T, preferred_element_type=jnp.float32).astype(jnp.bfloat16)
    half_done = half_done.reshape(NCHOL, NOCC, NAO)
    back_transformed = jnp.einsum("mi,kin->kmn", occupied_orbitals.astype(jnp.float32), half_done.astype(jnp.float32)).astype(jnp.bfloat16)
    blocked = gamma.reshape(NCHOL, NOCC, NVIR).astype(jnp.float32)
    vectors = cholesky.reshape(NCHOL, NOCC, NVIR).astype(jnp.float32)
    lagrangian = jnp.einsum("kib,kjb->ij", blocked, vectors) / NCHOL
    return back_transformed, lagrangian
```

```python
import functools

import jax
import jax.numpy as jnp
from jax import lax
from jax.experimental import pallas as pl
from jax.experimental.pallas import tpu as pltpu
from jax.sharding import PartitionSpec as P


LANES = 128
TILE_ROWS = 16
SUBLANES = 8
DEPTH_STEP = 3712
N_SPLIT = 3
NU_BLOCK = 256
OUT_PARTS = 3


def general_plan(n_vectors, density, cholesky, virtual_orbitals, occupied_orbitals):
    partial_value = jnp.dot(
        lax.all_gather(cholesky, "pair", axis=0, tiled=True),
        density,
        preferred_element_type=jnp.float32,
    )
    n_pair = lax.axis_size("pair")
    n_aux = lax.axis_size("aux")
    total_rows = partial_value.shape[0]
    per_group = total_rows // (n_pair * n_aux)
    arranged = partial_value.reshape(n_pair, n_aux, per_group, partial_value.shape[1])
    arranged = arranged.transpose(1, 0, 2, 3).reshape(total_rows, partial_value.shape[1])
    shared_part = lax.psum_scatter(arranged, "aux", scatter_dimension=0, tiled=True)
    pieces = lax.all_to_all(
        shared_part.astype(jnp.bfloat16), "pair", split_axis=0, concat_axis=1, tiled=True
    )
    vectors = lax.all_gather(pieces, "aux", axis=0, tiled=True)
    occupied = occupied_orbitals.shape[1]
    virtual = virtual_orbitals.shape[1]
    blocked = vectors.reshape(vectors.shape[0], occupied, virtual)
    half_done = jnp.einsum(
        "kia,na->kin", blocked, virtual_orbitals, preferred_element_type=jnp.float32
    ).astype(jnp.bfloat16)
    back_transformed = jnp.einsum(
        "mi,kin->kmn", occupied_orbitals, half_done, preferred_element_type=jnp.float32
    ).astype(jnp.bfloat16)
    local_vectors = cholesky.reshape(cholesky.shape[0], cholesky.shape[1] // virtual, virtual)
    lag_terms = (
        jnp.einsum("kib,kjb->ij", blocked, local_vectors, preferred_element_type=jnp.float32)
        / n_vectors
    )
    lagrangian = lax.psum(lag_terms, "pair")
    return (back_transformed, lagrangian)


def in_vmem(x):
    return pltpu.with_memory_space_constraint(x, pltpu.VMEM)


def contract_kernel(n_pieces, half, steps, last, aux_ref, *refs):
    pieces, d_ref = refs[:n_pieces], refs[n_pieces]
    keep_ref, send_ref, total_ref = refs[n_pieces + 1 :]
    depth = d_ref.shape[1]
    k = pl.program_id(0)

    def term(width):
        window = pl.ds(pl.multiple_of(k * depth, LANES), width)
        rows = jnp.concatenate(
            [p[h * half : (h + 1) * half, window] for h in range(2) for p in pieces], 0
        )
        return lax.dot_general(
            d_ref[:, :width], rows, (((1,), (1,)), ((), ())),
            preferred_element_type=jnp.float32,
        )

    @pl.when(k == 0)
    def _():
        total_ref[...] = term(depth)

    @pl.when((k > 0) & (k < steps - 1))
    def _():
        total_ref[...] += term(depth)

    @pl.when(k == steps - 1)
    def _():
        total = (total_ref[...] + term(last)).T
        split = n_pieces * half
        first = aux_ref[0] == 0
        keep_ref[...] = jnp.where(first, total[:split], total[split:])
        send_ref[...] = jnp.where(first, total[split:], total[:split])


def contract(aux, pieces, density_t, part, width):
    rows, depth = pieces[0].shape
    half = rows // 2
    steps = pl.cdiv(depth, DEPTH_STEP)
    last = depth - (steps - 1) * DEPTH_STEP
    out_rows = len(pieces) * half
    out = jax.ShapeDtypeStruct((out_rows, width), jnp.float32)
    out_spec = pl.BlockSpec((out_rows, width), lambda k, aux_ref: (0, 0))
    return pl.pallas_call(
        functools.partial(contract_kernel, len(pieces), half, steps, last),
        grid_spec=pltpu.PrefetchScalarGridSpec(
            num_scalar_prefetch=1,
            grid=(steps,),
            in_specs=[pl.BlockSpec(memory_space=pltpu.VMEM)] * len(pieces)
            + [pl.BlockSpec((width, DEPTH_STEP), lambda k, aux_ref: (part, k))],
            out_specs=[out_spec, out_spec],
            scratch_shapes=[pltpu.VMEM((width, 2 * out_rows), jnp.float32)],
        ),
        out_shape=[out, out],
        compiler_params=pltpu.CompilerParams(vmem_limit_bytes=24 << 20),
        cost_estimate=pl.CostEstimate(
            flops=2 * 2 * out_rows * depth * width,
            bytes_accessed=depth * width * 2,
            transcendentals=0,
        ),
    )(aux, *pieces, density_t)


def transform_kernel(n_groups, aux_ref, *refs):
    groups = refs[: 2 * n_groups]
    c_ref, w_ref, out_ref = refs[2 * n_groups], refs[2 * n_groups + 1], refs[-1]
    half = groups[0].shape[1]
    flat = jnp.concatenate([g[...].reshape(-1, g.shape[-1]) for g in groups], 0)
    product = jnp.dot(flat, c_ref[...], preferred_element_type=jnp.float32)
    width = product.shape[0] // 2
    for side in range(2):
        place = jnp.where(side == 0, aux_ref[0], 1 - aux_ref[0]) * half
        half_done = product[side * width : (side + 1) * width].T
        half_done = half_done.astype(jnp.bfloat16).astype(jnp.float32)
        n = half_done.shape[0]
        spread = jnp.broadcast_to(half_done[:, None, :], (n, SUBLANES, width))
        row = lax.broadcasted_iota(jnp.int32, (n, SUBLANES, width), 1)
        lane = lax.broadcasted_iota(jnp.int32, (n, SUBLANES, width), 2)
        picked = jnp.where(lax.rem(lane, SUBLANES) == row, spread, 0.0)
        picked = picked.reshape(n * SUBLANES, width).astype(jnp.bfloat16)
        result = jnp.dot(picked, w_ref[...], preferred_element_type=jnp.float32)
        result = result.reshape(n, SUBLANES, result.shape[1])
        ao_rows = out_ref.shape[2]
        result = jnp.concatenate([result[:, :, :ao_rows], result[:, :, ao_rows:]], 1)
        out_ref[:, pl.ds(pl.multiple_of(place, half), half), :] = result.astype(jnp.bfloat16)


def transform(aux, groups, virtual_t, weights, first_block, n_blocks, before=None):
    virtual, n_nu = virtual_t.shape
    half = groups[0].shape[1]
    ao_rows = weights.shape[1] // 2
    more = [] if before is None else [before]
    done = min(n_nu - first_block * NU_BLOCK, n_blocks * NU_BLOCK)
    return pl.pallas_call(
        functools.partial(transform_kernel, len(groups) // 2),
        grid_spec=pltpu.PrefetchScalarGridSpec(
            num_scalar_prefetch=1,
            grid=(n_blocks,),
            in_specs=[pl.BlockSpec(memory_space=pltpu.VMEM)] * len(groups)
            + [
                pl.BlockSpec((virtual, NU_BLOCK), lambda j, aux_ref: (0, j + first_block)),
                pl.BlockSpec(memory_space=pltpu.VMEM),
            ]
            + [pl.BlockSpec(memory_space=pl.ANY)] * len(more),
            out_specs=pl.BlockSpec(
                (NU_BLOCK, 2 * half, ao_rows), lambda j, aux_ref: (j + first_block, 0, 0)
            ),
        ),
        out_shape=jax.ShapeDtypeStruct((n_nu, 2 * half, ao_rows), jnp.bfloat16),
        input_output_aliases={len(groups) + 3: 0} if more else {},
        compiler_params=pltpu.CompilerParams(vmem_limit_bytes=32 << 20),
        cost_estimate=pl.CostEstimate(
            flops=2 * done * weights.shape[0] * (2 * virtual + SUBLANES * 2 * ao_rows),
            bytes_accessed=done * 2 * half * ao_rows * 2,
            transcendentals=0,
        ),
    )(aux, *groups, virtual_t, weights, *more)


def ring_plan(n_vectors, density, cholesky, virtual_orbitals, occupied_orbitals):
    n_pair = lax.axis_size("pair")
    chips = n_pair // 2
    columns = density.shape[1]
    virtual = virtual_orbitals.shape[1]
    occupied = occupied_orbitals.shape[1]
    per_device = columns // virtual
    rows = cholesky.shape[0]
    half = rows // 2
    order = list(range(0, chips, 2)) + list(range(1, chips, 2))[::-1]
    place = {chip: i for i, chip in enumerate(order)}

    def at(pair_index, distance):
        chip, core = divmod(pair_index, 2)
        step = distance if core == 0 else -distance
        return 2 * order[(place[chip] + step) % chips] + core

    sibling = [(p, p ^ 1) for p in range(n_pair)]
    swap = [(0, 1), (1, 0)]
    pair = lax.axis_index("pair")
    aux = lax.axis_index("aux").astype(jnp.int32).reshape(1)
    density_t = density.T

    own = [cholesky]
    for _ in range(1, chips):
        own.append(lax.ppermute(own[-1], "pair", [(p, at(p, 1)) for p in range(n_pair)]))
    beside = [lax.ppermute(x, "pair", sibling) for x in own]
    own, beside = [in_vmem(x) for x in own], [in_vmem(x) for x in beside]

    n_groups = 2
    steps = chips // n_groups
    width = columns // N_SPLIT
    mine, other = [], []
    for g in range(n_groups):
        group = range(g * steps, (g + 1) * steps)
        pieces = [x[t] for t in group for x in (own, beside)]
        summed = []
        for part in range(N_SPLIT):
            keep, send = contract(aux, pieces, density_t, part, width)
            got = lax.ppermute(send, "aux", swap)
            summed.append((keep + got).astype(jnp.bfloat16))
        summed = jnp.concatenate(summed, 1).reshape(steps, 2, half, columns)
        from_sibling = lax.ppermute(summed[:, 1], "pair", sibling)
        returned = []
        for k, t in enumerate(group):
            message = jnp.stack([summed[k, 0], from_sibling[k]])
            if t:
                message = lax.ppermute(
                    message, "pair", [(at(p, t), p) for p in range(n_pair)]
                )
            returned.append(message)
        returned = jnp.stack(returned).reshape(steps * 2, half, per_device, virtual)
        returned = returned.transpose(0, 2, 1, 3).reshape(steps * 2 * per_device, half, virtual)
        mine.append(returned)
        other.append(lax.ppermute(returned, "aux", swap))

    table = [
        [
            q * per_device + r
            for t in range(chips)
            for s in range(2)
            for q in (at(p, t) ^ s,)
            for r in range(per_device)
        ]
        for p in range(n_pair)
    ]
    index = jnp.asarray(table, jnp.int32)[pair]
    one_hot = (index[:, None] == jnp.arange(occupied)[None, :]).astype(jnp.float32)
    picked = jnp.dot(
        one_hot.astype(jnp.bfloat16), occupied_orbitals.T, preferred_element_type=jnp.float32
    ).astype(jnp.bfloat16)
    same = jnp.eye(2, dtype=jnp.bfloat16)
    weights = jnp.broadcast_to(
        picked[:, None, None, None, :] * same[None, :, None, :, None],
        (occupied, 2, half // 2, 2, picked.shape[1]),
    ).reshape(occupied * half, 2 * picked.shape[1])

    local = cholesky.reshape(2, half, cholesky.shape[1] // virtual, virtual)
    local_mine = jnp.where(aux[0] == 0, local[0], local[1])
    local_other = jnp.where(aux[0] == 0, local[1], local[0])
    terms = jnp.concatenate(
        [
            jnp.einsum("ikb,kjb->ij", m, local_mine, preferred_element_type=jnp.float32)
            + jnp.einsum("ikb,kjb->ij", o, local_other, preferred_element_type=jnp.float32)
            for m, o in zip(mine, other)
        ],
        0,
    )
    terms = jnp.sum(one_hot[:, :, None] * terms[:, None, :], 0) / n_vectors
    groups = [in_vmem(x) for x in mine + other]
    blocks = pl.cdiv(virtual_orbitals.shape[0], NU_BLOCK)
    per_call = pl.cdiv(blocks, OUT_PARTS)
    out = None
    for first in range(0, blocks, per_call):
        out = transform(
            aux, groups, virtual_orbitals.T, weights, first, min(per_call, blocks - first), out
        )
    span = 1
    while span < n_pair:
        terms = terms + lax.ppermute(terms, "pair", [(p, p ^ span) for p in range(n_pair)])
        span *= 2
    return out.transpose(1, 2, 0), terms


def on_device(n_vectors, density, cholesky, virtual_orbitals, occupied_orbitals):
    n_pair, n_aux = lax.axis_size("pair"), lax.axis_size("aux")
    fits = (
        n_aux == 2
        and n_pair % 4 == 0
        and n_pair & (n_pair - 1) == 0
        and density.shape[1] % virtual_orbitals.shape[1] == 0
        and cholesky.shape[0] == 2 * TILE_ROWS
        and density.shape[1] % (N_SPLIT * SUBLANES) == 0
        and occupied_orbitals.shape[0] % LANES == 0
    )
    plan = ring_plan if fits else general_plan
    return plan(n_vectors, density, cholesky, virtual_orbitals, occupied_orbitals)


def solution(mesh):
    def whole(density, cholesky, virtual_orbitals, occupied_orbitals):
        return jax.shard_map(
            functools.partial(on_device, cholesky.shape[0]),
            mesh=mesh,
            in_specs=(P("aux", "pair"), P("pair", "aux"), P("aux", None), P()),
            out_specs=(P("pair", None, "aux"), P(None, "aux")),
            check_vma=False,
        )(density, cholesky, virtual_orbitals, occupied_orbitals)

    return whole
```
